256 devices in a mesh: path: 64 (over x, z_lo, y, core), shard: 4 (over z_hi).
Axes of the slice: x: 4, y: 4, z: 8 (z_hi: 4, z_lo: 2; z = z_hi * 2 + z_lo), core: 2. Of those that a mesh axis runs over, the one named last changes fastest.
Arguments:
- path_delta: float32 [64, 2, 512, 1024], P('path', None, 'shard'), may hold values from -500 to 500
- assign: int32 [64, 2], replicated, may hold values from 0 to 15
- params: float32 [32, 4, 128, 1024], P(None, 'shard', 'path'), may hold values from -6 to 6
- momentum: float32 [32, 4, 128, 1024], P(None, 'shard', 'path'), may hold values from -3 to 3
Outputs:
- path_params: float32 [64, 2, 512, 1024], P('path', None, 'shard')
- new_params: float32 [32, 4, 128, 1024], P(None, 'shard', 'path')
- new_momentum: float32 [32, 4, 128, 1024], P(None, 'shard', 'path')
The draws below stay inside these ranges and needn't reach their ends.
All inputs are finite; a program needn't handle non-finite values.
Results may differ from the reference program's by a relative error of at most 0.00007.
Values sent between devices are 32-bit elements; how exact they have to be, the bound alone decides.
A program may use at most 128 MiB of HBM per device.

```python
import math
import jax
import jax.numpy as jnp
import numpy as np
from jax import lax

D = 1024
LEVEL_MODULES = 16
LEVELS = 2
ROWS = 512
PATHS = 64
MODULES = 32
BLOCK = 128
N_SHARD = 4


def draw_path_delta(key, part):
    key_base = jax.random.fold_in(key, 11)
    key_cols = jax.random.fold_in(key, 12)
    shape = (PATHS, LEVELS, ROWS, D)
    ramp = jnp.arange(ROWS, dtype=jnp.float32) / float(ROWS - 1)
    row_scale = jnp.exp(ramp * math.log(10.0))
    col_scale = jnp.exp(jax.random.uniform(key_cols, (PATHS, LEVELS, 1, D), jnp.float32) * math.log(10.0))
    base = jnp.clip(jax.random.normal(key_base, shape, jnp.float32), -4.0, 4.0)
    return base * row_scale[None, None, :, None] * col_scale


def place_ends(result, own_key, smallest, high):
    shape = result.shape
    spot = [jax.random.randint(jax.random.fold_in(own_key, axis), (), 0, shape[axis]) for axis in range(len(shape))]
    result = result.at[tuple(spot)].set(smallest)
    longest = shape.index(max(shape))
    spot[longest] = (spot[longest] + 1) % shape[longest]
    return result.at[tuple(spot)].set(high)


def block_scale(stream_key, extent, shards, least, largest):
    factor_of = 1.0
    for dim, shards_of in shards:
        heights = jax.random.uniform(jax.random.fold_in(jax.random.fold_in(stream_key, 6), dim), (shards_of,), jnp.float32, least / len(shards), largest / len(shards))
        factor_of = factor_of * jnp.repeat(jnp.exp(heights), extent[dim] // shards_of).reshape((-1,) + (1,) * (len(extent) - 1 - dim))
    return factor_of


def cumulative_ranks(amount, lean):
    portions = [(1 << 20) // math.isqrt(standing ** lean) + 1 for standing in range(1, amount + 1)]
    scale = 1 + sum(portions) // (1 << 30)
    return np.cumsum(np.array([max(1, weight // scale) for weight in portions]))


def ranked_ids(key, dims, count, skew):
    grid = cumulative_ranks(count, skew)
    pick = jax.random.randint(jax.random.fold_in(key, 1), dims, 0, int(grid[count - 1]))
    grade = jnp.searchsorted(jnp.asarray(grid, jnp.int32), pick, side="right")
    return jax.random.permutation(jax.random.fold_in(key, 2), count)[grade].astype(jnp.int32)


def bell_draw(key, shape, spread, limit, pieces=(), kind=jnp.bfloat16):
    level = block_scale(key, shape, pieces, -0.22, 0.18) if pieces else 1.0
    result = jax.random.normal(key, shape, jnp.float32) * spread * level
    return jnp.minimum(jnp.maximum(result, -limit), limit).astype(kind)


def setup_inputs(seed: int = 0) -> dict:
    keys = jax.random.split(jax.random.key(seed), 5)
    path_delta = draw_path_delta(jax.random.fold_in(keys[4], 71), 0)
    assign = place_ends(ranked_ids(keys[1], (PATHS, LEVELS), LEVEL_MODULES, 2), jax.random.fold_in(keys[1], 3), 0, LEVEL_MODULES - 1).astype(jnp.int32)
    params = bell_draw(keys[2], (MODULES, N_SHARD, BLOCK, D), 1.0, 6.0, ((1, 4), (2, 64)), jnp.float32)
    momentum = bell_draw(keys[3], (MODULES, N_SHARD, BLOCK, D), 0.5, 3.0, ((1, 4), (2, 64)), jnp.float32)
    return {"path_delta": path_delta, "assign": assign, "params": params, "momentum": momentum}


outer_rate = 0.7
beta_coef = 0.9

def reference(path_delta, assign, params, momentum):
    norm_sq = lax.optimization_barrier(jnp.sum(path_delta * path_delta, axis=(1, 2, 3)))
    rescale = 1.0 / jnp.sqrt(norm_sq / (LEVELS * ROWS * D) + 1e-06)
    scaled = path_delta * rescale[:, None, None, None]
    offsets = (jnp.arange(LEVELS, dtype=jnp.int32) * LEVEL_MODULES).astype(jnp.int32)
    module_id = (assign + offsets[None, :]).astype(jnp.int32)
    flat_ids = module_id.reshape(-1)
    sharers = lax.optimization_barrier(jnp.sum((flat_ids[:, None] == jnp.arange(MODULES, dtype=jnp.int32)[None, :]).astype(jnp.int32), axis=0))
    totals = jax.ops.segment_sum(scaled.reshape(PATHS * LEVELS, ROWS * D), flat_ids, num_segments=MODULES)
    divisor = jnp.maximum(sharers, 1).astype(totals.dtype)
    outer_grad = (totals / divisor[:, None]).reshape(MODULES, N_SHARD, BLOCK, D)
    new_momentum = beta_coef * momentum + outer_grad
    new_params = params - outer_rate * (outer_grad + beta_coef * new_momentum)
    path_params = jnp.take(new_params.reshape(MODULES, ROWS, D), flat_ids, axis=0).reshape(PATHS, LEVELS, ROWS, D)
    return (path_params, new_params, new_momentum)
```

```python
import jax
import jax.numpy as jnp
from jax import lax
from jax.experimental import pallas as pl
from jax.experimental.pallas import tpu as pltpu
from jax.sharding import PartitionSpec as P

LEVEL_MODULES = 16
LEVELS = 2
PATHS = 64
SHARDS = 4
MODULES = 32
STRIDE = 37

outer_rate = 0.7
beta_coef = 0.9

MESH = pl.DeviceIdType.MESH
f32 = jnp.float32
i32 = jnp.int32


def rem(a, b):
    return lax.rem(a, jnp.int32(b))


def div(a, b):
    return lax.div(a, jnp.int32(b))


def split(p):
    return div(p, 16), rem(div(p, 8), 2), rem(div(p, 2), 4), rem(p, 2)


def step_peers(me, i):
    x, z, y, c = split(me)
    dx, dz, dy, dc = split(rem(i * STRIDE, PATHS))
    to = rem(x + dx, 4) * 16 + rem(z + dz, 2) * 8 + rem(y + dy, 4) * 2 + rem(c + dc, 2)
    frm = rem(x + 4 - dx, 4) * 16 + rem(z + 2 - dz, 2) * 8 + rem(y + 4 - dy, 4) * 2 + rem(c + 2 - dc, 2)
    return to, frm


def kernel(
    x_send, x_sum, assign_ref, par_hbm, mom_hbm,
    ret_ref, newp_hbm, newm_hbm,
    xbuf, par, mom, newp, newm, landed, chain, outgoing,
    own_sq, sq_in, sq_row, sq_shards, itab, ftab, itab_s, ftab_s,
    lsem, sq_send, sq_recv, sh_send, sh_recv, d_send, d_recv, r_send, r_recv, own_sem,
):
    me = lax.axis_index("path")
    shard = lax.axis_index("shard")

    barrier = pltpu.get_barrier_semaphore()

    def greet(i, carry):
        to, _ = step_peers(me, i)
        pl.semaphore_signal(barrier, inc=1, device_id=(to, shard), device_id_type=MESH)
        return carry

    load_x = pltpu.make_async_copy(x_sum, xbuf, lsem.at[0])
    load_p = pltpu.make_async_copy(par_hbm, par, lsem.at[1])
    load_m = pltpu.make_async_copy(mom_hbm, mom, lsem.at[2])
    load_x.start()
    lax.fori_loop(1, PATHS, greet, 0)
    for k in range(1, SHARDS):
        pl.semaphore_signal(barrier, inc=1, device_id=(me, rem(shard + k, SHARDS)), device_id_type=MESH)
    load_p.start()
    load_m.start()

    rows = lax.broadcasted_iota(i32, (PATHS, PATHS), 0)
    lanes = lax.broadcasted_iota(i32, (PATHS, PATHS), 1)
    x, z, y, c = split(me)
    off = (rows * STRIDE) & (PATHS - 1)
    frm = (
        ((x - (off >> 4)) & 3) * 16
        + ((z - ((off >> 3) & 1)) & 1) * 8
        + ((y - ((off >> 1) & 3)) & 3) * 2
        + ((c - (off & 1)) & 1)
    )
    for l in range(LEVELS):
        a_row = assign_ref[l : l + 1, :]
        a_col = jnp.sum(jnp.where(frm == lanes, jnp.broadcast_to(a_row, (PATHS, PATHS)), 0), axis=1, keepdims=True)
        a_mat = jnp.broadcast_to(a_col, (PATHS, PATHS))
        a_by_step = jnp.sum(jnp.where(rows == lanes, a_mat, 0), axis=0, keepdims=True)
        same = (a_mat == jnp.broadcast_to(a_by_step, (PATHS, PATHS))) & (rows < lanes)
        before = jnp.max(jnp.where(same, rows + 1, 0), axis=0, keepdims=True)
        mine = a_mat == lanes
        last = jnp.max(jnp.where(mine, rows + 1, 0), axis=0, keepdims=True)
        count = jnp.sum(jnp.where(mine, 1.0, 0.0).astype(f32), axis=0, keepdims=True)
        itab[l : l + 1, 0:PATHS] = before
        itab[2 + l : 3 + l, 0:PATHS] = last
        itab[4 + l : 5 + l, 0:PATHS] = a_row
        ftab[1 + l : 2 + l, 0:PATHS] = 1.0 / jnp.maximum(count, 1.0)
    ints = pltpu.make_async_copy(itab, itab_s, lsem.at[3])
    ints.start()

    load_x.wait()

    def square(i, acc):
        part = xbuf[pl.ds(i * 16, 16)]
        part = part * part
        return acc + jnp.sum(part.reshape(4, 4, 8, 128), axis=0)

    acc = lax.fori_loop(0, 16, square, jnp.zeros((4, 8, 128), f32))
    total = jnp.sum(acc)
    own_sq[...] = jnp.broadcast_to(total, (1, 128))
    for l in range(LEVELS):
        chain[l, 0] = jnp.zeros((16, 128), f32)

    pl.semaphore_wait(barrier, PATHS - 1 + SHARDS - 1)

    def send_sq(i, carry):
        to, _ = step_peers(me, i)
        pltpu.make_async_remote_copy(
            own_sq, sq_in.at[i - 1], sq_send, sq_recv, device_id=(to, shard), device_id_type=MESH
        ).start()
        return carry

    lax.fori_loop(1, PATHS, send_sq, 0)

    def send_delta(i, carry):
        to, _ = step_peers(me, i)
        pltpu.make_async_remote_copy(
            x_send.at[:, div(to, 4), :, rem(to, 4)], landed.at[i], d_send, d_recv.at[i],
            device_id=(to, shard), device_id_type=MESH,
        ).start()
        return carry

    lax.fori_loop(1, PATHS, send_delta, 0)
    own = pltpu.make_async_copy(x_send.at[:, div(me, 4), :, rem(me, 4)], landed.at[0], own_sem.at[0])
    own.start()

    pltpu.make_async_copy(sq_in, sq_in, sq_recv).wait()
    lane = lax.broadcasted_iota(i32, (1, 128), 1)
    row = jnp.where(lane == 0, own_sq[...], 0.0)
    for i in range(1, PATHS):
        row = row + jnp.where(lane == i, sq_in[i - 1], 0.0)
    sq_row[...] = row
    ints.wait()
    copies = []
    for k in range(1, SHARDS):
        copy = pltpu.make_async_remote_copy(
            sq_row, sq_shards.at[k - 1], sh_send.at[k - 1], sh_recv.at[k - 1],
            device_id=(me, rem(shard + k, SHARDS)), device_id_type=MESH,
        )
        copy.start()
        copies.append(copy)
    for copy in copies:
        copy.wait_recv()
    norm = row + sq_shards[0] + sq_shards[1] + sq_shards[2]
    ftab[0:1, :] = 1.0 / jnp.sqrt(norm / (LEVELS * 512 * 1024) + 1e-06)
    floats = pltpu.make_async_copy(ftab, ftab_s, lsem.at[4])
    floats.start()
    floats.wait()

    arrived = landed.reshape(PATHS, LEVELS, 16, 128)

    def link(i):
        s = ftab_s[0, i]
        for l in range(LEVELS):
            chain[l, i + 1] = arrived[i, l] * s + chain[l, itab_s[l, i]]

    own.wait()
    link(0)

    def add(i, carry):
        pltpu.make_async_copy(landed.at[i], landed.at[i], d_recv.at[i]).wait()
        link(i)
        return carry

    lax.fori_loop(1, PATHS, add, 0)

    load_p.wait()
    load_m.wait()
    for l in range(LEVELS):
        def update(m, carry, l=l):
            grad = chain[l, itab_s[2 + l, m]] * ftab_s[1 + l, m]
            k = l * LEVEL_MODULES + m
            moment = beta_coef * mom[k] + grad
            newm[k] = moment
            newp[k] = par[k] - outer_rate * (grad + beta_coef * moment)
            return carry

        lax.fori_loop(0, LEVEL_MODULES, update, 0, unroll=4)
    put_p = pltpu.make_async_copy(newp, newp_hbm, lsem.at[5])
    put_m = pltpu.make_async_copy(newm, newm_hbm, lsem.at[6])
    put_p.start()
    put_m.start()

    out_view = outgoing.reshape(PATHS, LEVELS, 16, 128)

    def pick(i, carry):
        to, _ = step_peers(me, i)
        for l in range(LEVELS):
            out_view[i, l] = newp[l * LEVEL_MODULES + itab_s[4 + l, to]]
        return carry

    lax.fori_loop(0, PATHS, pick, 0, unroll=4)

    def send_back(i, carry):
        to, _ = step_peers(me, i)
        pltpu.make_async_remote_copy(
            outgoing.at[i], ret_ref.at[:, div(me, 4), :, rem(me, 4)], r_send, r_recv,
            device_id=(to, shard), device_id_type=MESH,
        ).start()
        return carry

    lax.fori_loop(1, PATHS, send_back, 0)
    keep = pltpu.make_async_copy(outgoing.at[0], ret_ref.at[:, div(me, 4), :, rem(me, 4)], own_sem.at[1])
    keep.start()

    for copy in copies:
        copy.wait_send()
    pltpu.make_async_copy(sq_in, sq_in, sq_send).wait()
    rest = outgoing.at[pl.ds(1, PATHS - 1)]
    pltpu.make_async_copy(rest, rest, d_send).wait()
    keep.wait()
    put_p.wait()
    put_m.wait()
    pltpu.make_async_copy(rest, rest, r_send).wait()
    pltpu.make_async_copy(rest, rest, r_recv).wait()


def local(path_delta, assign, params, momentum):
    x_sum = path_delta[0].reshape(2, 16, 8, 8, 128).transpose(0, 1, 3, 2, 4)
    x_send = x_sum.reshape(2, 16, 8, 4, 2, 128)
    x_sum = x_sum.reshape(256, 8, 128)

    def rows_of(a):
        return a.reshape(MODULES, 2, 8, 128).transpose(0, 2, 1, 3).reshape(MODULES, 16, 128)

    def back(a):
        return a.reshape(MODULES, 8, 2, 128).transpose(0, 2, 1, 3).reshape(MODULES, 1, 2, 1024)

    any_space = pl.BlockSpec(memory_space=pl.ANY)
    vm = pltpu.VMEM
    slab = (MODULES, 16, 128)
    dma = pltpu.SemaphoreType.DMA
    ret, newp, newm = pl.pallas_call(
        kernel,
        out_shape=(
            jax.ShapeDtypeStruct((2, 16, 8, 4, 2, 128), f32),
            jax.ShapeDtypeStruct(slab, f32),
            jax.ShapeDtypeStruct(slab, f32),
        ),
        in_specs=[any_space, any_space, pl.BlockSpec(memory_space=pltpu.VMEM), any_space, any_space],
        out_specs=(any_space, any_space, any_space),
        scratch_shapes=[
            vm((256, 8, 128), f32), vm(slab, f32), vm(slab, f32), vm(slab, f32), vm(slab, f32),
            vm((PATHS, LEVELS, 8, 2, 128), f32), vm((LEVELS, PATHS + 1, 16, 128), f32),
            vm((PATHS, LEVELS, 8, 2, 128), f32),
            vm((1, 128), f32), vm((PATHS - 1, 1, 128), f32), vm((1, 128), f32), vm((SHARDS - 1, 1, 128), f32),
            vm((8, 128), i32), vm((8, 128), f32), pltpu.SMEM((8, 128), i32), pltpu.SMEM((8, 128), f32),
            dma((7,)), dma, dma, dma((SHARDS - 1,)), dma((SHARDS - 1,)), dma, dma((PATHS,)), dma, dma, dma((2,)),
        ],
        compiler_params=pltpu.CompilerParams(
            collective_id=1, has_side_effects=True, vmem_limit_bytes=32 * 2**20
        ),
        name="outer_step",
    )(x_send, x_sum, assign.T, rows_of(params[:, 0]), rows_of(momentum[:, 0]))
    path_params = ret.reshape(2, 16, 8, 8, 128).transpose(0, 1, 3, 2, 4).reshape(1, 2, 128, 1024)
    return path_params, back(newp), back(newm)


def solution(mesh):
    in_specs = (
        P("path", None, "shard", None),
        P(),
        P(None, "shard", "path", None),
        P(None, "shard", "path", None),
    )
    out_specs = (
        P("path", None, "shard", None),
        P(None, "shard", "path", None),
        P(None, "shard", "path", None),
    )
    return jax.shard_map(local, mesh=mesh, in_specs=in_specs, out_specs=out_specs, check_vma=False)
```

```python
import jax
import jax.numpy as jnp
from jax import lax
from jax.experimental import pallas as pl
from jax.experimental.pallas import tpu as pltpu
from jax.sharding import PartitionSpec as P

LEVEL_MODULES = 16
LEVELS = 2
PATHS = 64
SHARDS = 4
MODULES = 32
STRIDE = 37
CHUNKS = 2
EARLY = 63
GROUP = 16

outer_rate = 0.7
beta_coef = 0.9

MESH = pl.DeviceIdType.MESH
f32 = jnp.float32
i32 = jnp.int32
WIDE = 8 // CHUNKS
SUB = 2 * WIDE


def digits(p):
    return p // 16, p // 8 % 2, p // 2 % 4, p % 2


class Peers:
    def __init__(self, me):
        rem, div = lax.rem, lax.div
        x, z, y, c = div(me, 16), rem(div(me, 8), 2), rem(div(me, 2), 4), rem(me, 2)
        self.xs = [rem(x + d, 4) for d in range(4)]
        self.zs = [rem(z + d, 2) for d in range(2)]
        self.cs = [rem(c + d, 2) for d in range(2)]
        ys = [rem(y + d, 4) for d in range(4)]
        self.xz = [[a * 16 + b * 8 for b in self.zs] for a in self.xs]
        self.xz_tile = [[a * 4 + b * 2 for b in self.zs] for a in self.xs]
        self.yc = [[a * 2 + b for b in self.cs] for a in ys]
        self.y_tile = [div(a, 2) for a in ys]
        self.yc_pair = [[rem(a, 2) * 2 + b for b in self.cs] for a in ys]

    def to(self, i):
        dx, dz, dy, dc = digits(i * STRIDE % PATHS)
        return self.xz[dx][dz] + self.yc[dy][dc]

    def place(self, i):
        dx, dz, dy, dc = digits(i * STRIDE % PATHS)
        return self.xz_tile[dx][dz] + self.y_tile[dy], self.yc_pair[dy][dc]


def kernel(
    x_send, x_sum, assign_hbm, par_hbm, mom_hbm,
    ret_ref, newp_ref, newm_ref,
    assign_ref, xbuf, par, mom, newp, newm, landed, chain, outgoing,
    own_sq, sq_in, sq_row, sq_shards, itab, ftab, itab_s, ftab_s,
    lsem, sq_send, sq_recv, sh_send, sh_recv, d_send, d_recv, r_send, r_recv, own_sem,
):
    me = lax.axis_index("path")
    shard = lax.axis_index("shard")
    peers = Peers(me)
    shard_peers = [lax.rem(shard + k, SHARDS) for k in range(SHARDS)]
    steps = range(1, PATHS)

    barrier = pltpu.get_barrier_semaphore()
    for i in steps:
        pl.semaphore_signal(barrier, inc=1, device_id=(peers.to(i), shard), device_id_type=MESH)
    for k in range(1, SHARDS):
        pl.semaphore_signal(barrier, inc=1, device_id=(me, shard_peers[k]), device_id_type=MESH)

    load_x = pltpu.make_async_copy(x_sum, xbuf, lsem.at[0])
    load_a = pltpu.make_async_copy(assign_hbm, assign_ref, lsem.at[3])
    load_p = pltpu.make_async_copy(par_hbm, par, lsem.at[1])
    load_m = pltpu.make_async_copy(mom_hbm, mom, lsem.at[2])
    for copy in (load_x, load_a, load_p, load_m):
        copy.start()

    load_a.wait()
    rows = lax.broadcasted_iota(i32, (PATHS, PATHS), 0)
    lanes = lax.broadcasted_iota(i32, (PATHS, PATHS), 1)
    x, z, y, c = lax.div(me, 16), lax.rem(lax.div(me, 8), 2), lax.rem(lax.div(me, 2), 4), lax.rem(me, 2)
    off = (rows * STRIDE) & (PATHS - 1)
    frm = (
        ((x - (off >> 4)) & 3) * 16
        + ((z - ((off >> 3) & 1)) & 1) * 8
        + ((y - ((off >> 1) & 3)) & 3) * 2
        + ((c - (off & 1)) & 1)
    )
    for l in range(LEVELS):
        a_row = assign_ref[l : l + 1, :]
        a_col = jnp.sum(jnp.where(frm == lanes, jnp.broadcast_to(a_row, (PATHS, PATHS)), 0), axis=1, keepdims=True)
        a_mat = jnp.broadcast_to(a_col, (PATHS, PATHS))
        a_by_step = jnp.sum(jnp.where(rows == lanes, a_mat, 0), axis=0, keepdims=True)
        same = (a_mat == jnp.broadcast_to(a_by_step, (PATHS, PATHS))) & (rows < lanes)
        before = jnp.max(jnp.where(same, rows + 1, 0), axis=0, keepdims=True)
        mine = a_mat == lanes
        last = jnp.max(jnp.where(mine, rows + 1, 0), axis=0, keepdims=True)
        count = jnp.sum(jnp.where(mine, 1.0, 0.0).astype(f32), axis=0, keepdims=True)
        itab[l : l + 1, 0:PATHS] = before
        itab[2 + l : 3 + l, 0:PATHS] = last
        itab[4 + l : 5 + l, 0:PATHS] = a_row
        ftab[1 + l : 2 + l, 0:PATHS] = 1.0 / jnp.maximum(count, 1.0)
    ints = pltpu.make_async_copy(itab, itab_s, lsem.at[3])
    ints.start()

    load_x.wait()

    def square(i, acc):
        part = xbuf[pl.ds(i * 16, 16)]
        part = part * part
        return acc + jnp.sum(part.reshape(4, 4, 8, 128), axis=0)

    acc = lax.fori_loop(0, 16, square, jnp.zeros((4, 8, 128), f32))
    own_sq[...] = jnp.broadcast_to(jnp.sum(acc), (1, 128))
    for h in range(CHUNKS):
        for l in range(LEVELS):
            chain[h, l, 0] = jnp.zeros((SUB, 128), f32)
    ints.wait()

    pl.semaphore_wait(barrier, PATHS - 1 + SHARDS - 1)

    for i in steps:
        pltpu.make_async_remote_copy(
            own_sq, sq_in.at[i - 1], sq_send, sq_recv, device_id=(peers.to(i), shard), device_id_type=MESH
        ).start()

    def send_delta(h, i):
        tile, pair = peers.place(i)
        pltpu.make_async_remote_copy(
            x_send.at[:, tile, pl.ds(h * WIDE, WIDE), pair], landed.at[h, i], d_send, d_recv.at[h, i],
            device_id=(peers.to(i), shard), device_id_type=MESH,
        ).start()

    order = [(h, i) for h in range(CHUNKS) for i in steps]
    for h, i in order[:EARLY]:
        send_delta(h, i)
    tile, pair = peers.place(0)
    own = [
        pltpu.make_async_copy(x_send.at[:, tile, pl.ds(h * WIDE, WIDE), pair], landed.at[h, 0], own_sem.at[h])
        for h in range(CHUNKS)
    ]
    for copy in own:
        copy.start()

    pltpu.make_async_copy(sq_in, sq_in, sq_recv).wait()
    lane = lax.broadcasted_iota(i32, (1, 128), 1)
    part = [jnp.where(lane == 0, own_sq[...], 0.0)] + [jnp.where(lane == i, sq_in[i - 1], 0.0) for i in steps]
    while len(part) > 1:
        part = [a + b for a, b in zip(part[::2], part[1::2])]
    row = part[0]
    sq_row[...] = row
    copies = [
        pltpu.make_async_remote_copy(
            sq_row, sq_shards.at[k - 1], sh_send.at[k - 1], sh_recv.at[k - 1],
            device_id=(me, shard_peers[k]), device_id_type=MESH,
        )
        for k in range(1, SHARDS)
    ]
    for copy in copies:
        copy.start()
    for h, i in order[EARLY:]:
        send_delta(h, i)
    for copy in copies:
        copy.wait_recv()
    norm = row + sq_shards[0] + sq_shards[1] + sq_shards[2]
    ftab[0:1, :] = 1.0 / jnp.sqrt(norm / (LEVELS * 512 * 1024) + 1e-06)
    floats = pltpu.make_async_copy(ftab, ftab_s, lsem.at[4])
    floats.start()
    floats.wait()
    load_p.wait()
    load_m.wait()

    arrived = landed.reshape(CHUNKS, PATHS, LEVELS, SUB, 128)
    out_view = outgoing.reshape(CHUNKS, PATHS, LEVELS, SUB, 128)
    my_tile, my_pair = peers.place(0)

    for h in range(CHUNKS):
        for i in range(PATHS):
            if i == 0:
                own[h].wait()
            else:
                pltpu.make_async_copy(landed.at[h, i], landed.at[h, i], d_recv.at[h, i]).wait()
            s = ftab_s[0, i]
            for l in range(LEVELS):
                chain[h, l, i + 1] = arrived[h, i, l] * s + chain[h, l, itab_s[l, i]]

        cols = pl.ds(h * SUB, SUB)
        for l in range(LEVELS):
            for m in range(LEVEL_MODULES):
                k = l * LEVEL_MODULES + m
                grad = chain[h, l, itab_s[2 + l, m]] * ftab_s[1 + l, m]
                moment = beta_coef * mom[k, cols] + grad
                newm[k, cols] = moment
                newp[k, cols] = par[k, cols] - outer_rate * (grad + beta_coef * moment)

        def pick(i):
            to = peers.to(i)
            for l in range(LEVELS):
                out_view[h, i, l] = newp[l * LEVEL_MODULES + itab_s[4 + l, to], cols]

        def send_back(i):
            dst = ret_ref.at[:, my_tile, pl.ds(h * WIDE, WIDE), my_pair]
            if i == 0:
                pltpu.make_async_copy(outgoing.at[h, i], dst, own_sem.at[CHUNKS + h]).start()
            else:
                pltpu.make_async_remote_copy(
                    outgoing.at[h, i], dst, r_send.at[h], r_recv.at[h],
                    device_id=(peers.to(i), shard), device_id_type=MESH,
                ).start()

        todo = [1 + i for i in range(PATHS - 1)] + [0]
        groups = [todo[g : g + GROUP] for g in range(0, PATHS, GROUP)]
        for g in range(len(groups) + 1):
            for i in groups[g] if g < len(groups) else ():
                pick(i)
            for i in groups[g - 1] if g > 0 else ():
                send_back(i)

    put_p = pltpu.make_async_copy(newp, newp_ref, lsem.at[5])
    put_m = pltpu.make_async_copy(newm, newm_ref, lsem.at[6])
    put_p.start()
    put_m.start()
    for copy in copies:
        copy.wait_send()
    pltpu.make_async_copy(sq_in, sq_in, sq_send).wait()
    for h in range(CHUNKS):
        rest = outgoing.at[h, pl.ds(1, PATHS - 1)]
        pltpu.make_async_copy(rest, rest, d_send).wait()
    put_p.wait()
    put_m.wait()
    for h in range(CHUNKS):
        rest = outgoing.at[h, pl.ds(1, PATHS - 1)]
        pltpu.make_async_copy(outgoing.at[h, 0], outgoing.at[h, 0], own_sem.at[CHUNKS + h]).wait()
        pltpu.make_async_copy(rest, rest, r_send.at[h]).wait()
        pltpu.make_async_copy(rest, rest, r_recv.at[h]).wait()


def finish(a, b, c, a_out, b_out, c_out, sem):
    copies = [pltpu.make_async_copy(s, d, sem.at[k]) for k, (s, d) in enumerate(((a, a_out), (b, b_out), (c, c_out)))]
    for copy in copies:
        copy.start()
    for copy in copies:
        copy.wait()


def local(path_delta, assign, params, momentum):
    x_sum = path_delta[0].reshape(2, 16, 8, 8, 128).transpose(0, 1, 3, 2, 4)
    x_send = x_sum.reshape(2, 16, 8, 4, 2, 128)
    x_sum = x_sum.reshape(256, 8, 128)

    def rows_of(a):
        return a.reshape(MODULES, 2, 8, 128).transpose(0, 2, 1, 3).reshape(MODULES, 16, 128)

    def back(a):
        return a.reshape(MODULES, 8, 2, 128).transpose(0, 2, 1, 3).reshape(MODULES, 1, 2, 1024)

    any_space = pl.BlockSpec(memory_space=pl.ANY)
    vm = pltpu.VMEM
    slab = (MODULES, 16, 128)
    dma = pltpu.SemaphoreType.DMA
    operands = (x_send, x_sum, assign.T, rows_of(params[:, 0]), rows_of(momentum[:, 0]))
    ret, newp, newm = pl.pallas_call(
        kernel,
        out_shape=(
            jax.ShapeDtypeStruct((2, 16, 8, 4, 2, 128), f32),
            jax.ShapeDtypeStruct(slab, f32),
            jax.ShapeDtypeStruct(slab, f32),
        ),
        in_specs=[any_space] * 5,
        out_specs=[any_space] * 3,
        scratch_shapes=[
            vm((LEVELS, PATHS), i32), vm((256, 8, 128), f32), vm(slab, f32), vm(slab, f32), vm(slab, f32), vm(slab, f32),
            vm((CHUNKS, PATHS, LEVELS, WIDE, 2, 128), f32), vm((CHUNKS, LEVELS, PATHS + 1, SUB, 128), f32),
            vm((CHUNKS, PATHS, LEVELS, WIDE, 2, 128), f32),
            vm((1, 128), f32), vm((PATHS - 1, 1, 128), f32), vm((1, 128), f32), vm((SHARDS - 1, 1, 128), f32),
            vm((8, 128), i32), vm((8, 128), f32), pltpu.SMEM((8, 128), i32), pltpu.SMEM((8, 128), f32),
            dma((7,)), dma, dma, dma((SHARDS - 1,)), dma((SHARDS - 1,)), dma, dma((CHUNKS, PATHS)),
            dma((CHUNKS,)), dma((CHUNKS,)), dma((2 * CHUNKS,)),
        ],
        compiler_params=pltpu.CompilerParams(
            collective_id=1, has_side_effects=True, vmem_limit_bytes=32 * 2**20
        ),
        name="outer_step",
    )(*[pltpu.with_memory_space_constraint(v, pltpu.HBM) for v in operands])
    outs = (ret.reshape(2, 16, 8, 8, 128), newp, newm)
    ret, newp, newm = pl.pallas_call(
        finish,
        out_shape=[jax.ShapeDtypeStruct(o.shape, o.dtype) for o in outs],
        in_specs=[any_space] * 3,
        out_specs=[any_space] * 3,
        scratch_shapes=[dma((3,))],
        compiler_params=pltpu.CompilerParams(vmem_limit_bytes=2**20),
        name="finish",
    )(*[pltpu.with_memory_space_constraint(v, pltpu.VMEM) for v in outs])
    path_params = ret.transpose(0, 1, 3, 2, 4).reshape(1, 2, 128, 1024)
    return path_params, back(newp), back(newm)


def solution(mesh):
    in_specs = (
        P("path", None, "shard", None),
        P(),
        P(None, "shard", "path", None),
        P(None, "shard", "path", None),
    )
    out_specs = (
        P("path", None, "shard", None),
        P(None, "shard", "path", None),
        P(None, "shard", "path", None),
    )
    return jax.shard_map(local, mesh=mesh, in_specs=in_specs, out_specs=out_specs, check_vma=False)
```

```python
import jax
import jax.numpy as jnp
from jax import lax
from jax.experimental import pallas as pl
from jax.experimental.pallas import tpu as pltpu
from jax.sharding import PartitionSpec as P

LEVEL_MODULES = 16
LEVELS = 2
PATHS = 64
SHARDS = 4
MODULES = 32
CHUNKS = 2
EARLY = 63
GROUP = 16

outer_rate = 0.7
beta_coef = 0.9

MESH = pl.DeviceIdType.MESH
f32 = jnp.float32
i32 = jnp.int32
WIDE = 8 // CHUNKS
SUB = 2 * WIDE


def digits(p):
    return p // 16, p // 8 % 2, p // 2 % 4, p % 2


def links(offset):
    x, z, y, _ = digits(offset)
    ring = {0: (0, 0), 1: (1, 0), 2: (1, 1), 3: (0, 1)}
    return (*ring[x], *ring[y], z)


def far_first():
    left, load, order = list(range(1, PATHS)), (0,) * 5, [0]

    def cost(o):
        total = [a + b for a, b in zip(load, links(o))]
        return -sum(links(o)), max(total) - min(total), o * 45 % PATHS

    while left:
        o = min(left, key=cost)
        left.remove(o)
        order.append(o)
        load = tuple(a + b for a, b in zip(load, links(o)))
    return order


OFFSETS = far_first()


class Peers:
    def __init__(self, me):
        rem, div = lax.rem, lax.div
        x, z, y, c = div(me, 16), rem(div(me, 8), 2), rem(div(me, 2), 4), rem(me, 2)
        self.xs = [rem(x + d, 4) for d in range(4)]
        self.zs = [rem(z + d, 2) for d in range(2)]
        self.cs = [rem(c + d, 2) for d in range(2)]
        ys = [rem(y + d, 4) for d in range(4)]
        self.xz = [[a * 16 + b * 8 for b in self.zs] for a in self.xs]
        self.xz_tile = [[a * 4 + b * 2 for b in self.zs] for a in self.xs]
        self.yc = [[a * 2 + b for b in self.cs] for a in ys]
        self.y_tile = [div(a, 2) for a in ys]
        self.yc_pair = [[rem(a, 2) * 2 + b for b in self.cs] for a in ys]

    def to(self, i):
        dx, dz, dy, dc = digits(OFFSETS[i])
        return self.xz[dx][dz] + self.yc[dy][dc]

    def place(self, i):
        dx, dz, dy, dc = digits(OFFSETS[i])
        return self.xz_tile[dx][dz] + self.y_tile[dy], self.yc_pair[dy][dc]


def kernel(
    x_send, x_sum, assign_hbm, par_hbm, mom_hbm,
    ret_ref, newp_ref, newm_ref,
    assign_ref, xbuf, par, mom, newp, newm, landed, chain, outgoing,
    own_sq, sq_in, sq_row, sq_shards, itab, ftab, scale, itab_s, ftab_s,
    lsem, sq_send, sq_recv, sh_send, sh_recv, d_send, d_recv, r_send, r_recv, own_sem,
):
    me = lax.axis_index("path")
    shard = lax.axis_index("shard")
    peers = Peers(me)
    shard_peers = [lax.rem(shard + k, SHARDS) for k in range(SHARDS)]
    steps = range(1, PATHS)

    barrier = pltpu.get_barrier_semaphore()
    for i in steps[:32]:
        pl.semaphore_signal(barrier, inc=1, device_id=(peers.to(i), shard), device_id_type=MESH)
    for k in (2, 1, 3):
        pl.semaphore_signal(barrier, inc=1, device_id=(me, shard_peers[k]), device_id_type=MESH)
    for i in steps[32:]:
        pl.semaphore_signal(barrier, inc=1, device_id=(peers.to(i), shard), device_id_type=MESH)

    load_x = pltpu.make_async_copy(x_sum, xbuf, lsem.at[0])
    load_a = pltpu.make_async_copy(assign_hbm, assign_ref, lsem.at[3])
    load_p = pltpu.make_async_copy(par_hbm, par, lsem.at[1])
    load_m = pltpu.make_async_copy(mom_hbm, mom, lsem.at[2])
    for copy in (load_x, load_a, load_p, load_m):
        copy.start()

    load_a.wait()
    rows = lax.broadcasted_iota(i32, (PATHS, PATHS), 0)
    lanes = lax.broadcasted_iota(i32, (PATHS, PATHS), 1)
    x, z, y, c = lax.div(me, 16), lax.rem(lax.div(me, 8), 2), lax.rem(lax.div(me, 2), 4), lax.rem(me, 2)
    off = jnp.zeros((PATHS, PATHS), i32)
    for i in range(1, PATHS):
        off = jnp.where(rows == i, OFFSETS[i], off)
    frm = (
        ((x - (off >> 4)) & 3) * 16
        + ((z - ((off >> 3) & 1)) & 1) * 8
        + ((y - ((off >> 1) & 3)) & 3) * 2
        + ((c - (off & 1)) & 1)
    )
    for l in range(LEVELS):
        a_row = assign_ref[l : l + 1, :]
        a_col = jnp.sum(jnp.where(frm == lanes, jnp.broadcast_to(a_row, (PATHS, PATHS)), 0), axis=1, keepdims=True)
        a_mat = jnp.broadcast_to(a_col, (PATHS, PATHS))
        a_by_step = jnp.sum(jnp.where(rows == lanes, a_mat, 0), axis=0, keepdims=True)
        same = (a_mat == jnp.broadcast_to(a_by_step, (PATHS, PATHS))) & (rows < lanes)
        before = jnp.max(jnp.where(same, rows + 1, 0), axis=0, keepdims=True)
        mine = a_mat == lanes
        last = jnp.max(jnp.where(mine, rows + 1, 0), axis=0, keepdims=True)
        count = jnp.sum(jnp.where(mine, 1.0, 0.0).astype(f32), axis=0, keepdims=True)
        itab[l : l + 1, 0:PATHS] = before
        itab[2 + l : 3 + l, 0:PATHS] = last
        itab[4 + l : 5 + l, 0:PATHS] = a_row
        ftab[l : l + 1, 0:PATHS] = 1.0 / jnp.maximum(count, 1.0)
    ints = pltpu.make_async_copy(itab, itab_s, lsem.at[3])
    ints.start()
    floats = pltpu.make_async_copy(ftab, ftab_s, lsem.at[4])
    floats.start()

    load_x.wait()

    def square(i, acc):
        part = xbuf[pl.ds(i * 16, 16)]
        part = part * part
        return acc + jnp.sum(part.reshape(4, 4, 8, 128), axis=0)

    acc = lax.fori_loop(0, 16, square, jnp.zeros((4, 8, 128), f32))
    own_sq[...] = jnp.broadcast_to(jnp.sum(acc), (1, 128))
    for h in range(CHUNKS):
        for l in range(LEVELS):
            chain[h, l, 0] = jnp.zeros((SUB, 128), f32)
    ints.wait()
    floats.wait()

    pl.semaphore_wait(barrier, PATHS - 1 + SHARDS - 1)

    for i in steps:
        pltpu.make_async_remote_copy(
            own_sq, sq_in.at[i - 1], sq_send, sq_recv, device_id=(peers.to(i), shard), device_id_type=MESH
        ).start()

    def send_delta(h, i):
        tile, pair = peers.place(i)
        pltpu.make_async_remote_copy(
            x_send.at[:, tile, pl.ds(h * WIDE, WIDE), pair], landed.at[h, i], d_send, d_recv.at[h, i],
            device_id=(peers.to(i), shard), device_id_type=MESH,
        ).start()

    order = [(h, i) for h in range(CHUNKS) for i in steps]
    for h, i in order[:EARLY]:
        send_delta(h, i)
    tile, pair = peers.place(0)
    own = [
        pltpu.make_async_copy(x_send.at[:, tile, pl.ds(h * WIDE, WIDE), pair], landed.at[h, 0], own_sem.at[h])
        for h in range(CHUNKS)
    ]
    for copy in own:
        copy.start()

    pltpu.make_async_copy(sq_in, sq_in, sq_recv).wait()
    lane = lax.broadcasted_iota(i32, (1, 128), 1)
    part = [jnp.where(lane == 0, own_sq[...], 0.0)] + [jnp.where(lane == i, sq_in[i - 1], 0.0) for i in steps]
    while len(part) > 1:
        part = [a + b for a, b in zip(part[::2], part[1::2])]
    row = part[0]
    sq_row[...] = row
    copies = [
        pltpu.make_async_remote_copy(
            sq_row, sq_shards.at[k - 1], sh_send.at[k - 1], sh_recv.at[k - 1],
            device_id=(me, shard_peers[k]), device_id_type=MESH,
        )
        for k in range(1, SHARDS)
    ]
    for copy in copies:
        copy.start()
    for h, i in order[EARLY:]:
        send_delta(h, i)
    for copy in copies:
        copy.wait_recv()
    norm = row + sq_shards[0] + sq_shards[1] + sq_shards[2]
    rescale = 1.0 / jnp.sqrt(norm / (LEVELS * 512 * 1024) + 1e-06)
    spread = jnp.where(rows == lanes, jnp.broadcast_to(rescale[:, 0:PATHS], (PATHS, PATHS)), 0.0)
    scale[...] = jnp.broadcast_to(jnp.sum(spread, axis=1, keepdims=True), (PATHS, 128))
    load_p.wait()
    load_m.wait()

    arrived = landed.reshape(CHUNKS, PATHS, LEVELS, SUB, 128)
    out_view = outgoing.reshape(CHUNKS, PATHS, LEVELS, SUB, 128)
    my_tile, my_pair = peers.place(0)

    for h in range(CHUNKS):
        for i in range(PATHS):
            if i == 0:
                own[h].wait()
            else:
                pltpu.make_async_copy(landed.at[h, i], landed.at[h, i], d_recv.at[h, i]).wait()
            s = scale[i : i + 1, :]
            for l in range(LEVELS):
                chain[h, l, i + 1] = arrived[h, i, l] * s + chain[h, l, itab_s[l, i]]

        cols = pl.ds(h * SUB, SUB)
        for l in range(LEVELS):
            for m in range(LEVEL_MODULES):
                k = l * LEVEL_MODULES + m
                grad = chain[h, l, itab_s[2 + l, m]] * ftab_s[l, m]
                moment = beta_coef * mom[k, cols] + grad
                newm[k, cols] = moment
                newp[k, cols] = par[k, cols] - outer_rate * (grad + beta_coef * moment)

        def pick(i):
            to = peers.to(i)
            for l in range(LEVELS):
                out_view[h, i, l] = newp[l * LEVEL_MODULES + itab_s[4 + l, to], cols]

        def send_back(i):
            dst = ret_ref.at[:, my_tile, pl.ds(h * WIDE, WIDE), my_pair]
            if i == 0:
                pltpu.make_async_copy(outgoing.at[h, i], dst, own_sem.at[CHUNKS + h]).start()
            else:
                pltpu.make_async_remote_copy(
                    outgoing.at[h, i], dst, r_send.at[h], r_recv.at[h],
                    device_id=(peers.to(i), shard), device_id_type=MESH,
                ).start()

        todo = [1 + i for i in range(PATHS - 1)] + [0]
        groups = [todo[g : g + GROUP] for g in range(0, PATHS, GROUP)]
        for g in range(len(groups) + 1):
            for i in groups[g] if g < len(groups) else ():
                pick(i)
            for i in groups[g - 1] if g > 0 else ():
                send_back(i)

    put_p = pltpu.make_async_copy(newp, newp_ref, lsem.at[5])
    put_m = pltpu.make_async_copy(newm, newm_ref, lsem.at[6])
    put_p.start()
    put_m.start()
    for copy in copies:
        copy.wait_send()
    pltpu.make_async_copy(sq_in, sq_in, sq_send).wait()
    for h in range(CHUNKS):
        rest = outgoing.at[h, pl.ds(1, PATHS - 1)]
        pltpu.make_async_copy(rest, rest, d_send).wait()
    put_p.wait()
    put_m.wait()
    for h in range(CHUNKS):
        rest = outgoing.at[h, pl.ds(1, PATHS - 1)]
        pltpu.make_async_copy(outgoing.at[h, 0], outgoing.at[h, 0], own_sem.at[CHUNKS + h]).wait()
        pltpu.make_async_copy(rest, rest, r_send.at[h]).wait()
        pltpu.make_async_copy(rest, rest, r_recv.at[h]).wait()


def finish(a, b, c, a_out, b_out, c_out, sem):
    copies = [pltpu.make_async_copy(s, d, sem.at[k]) for k, (s, d) in enumerate(((a, a_out), (b, b_out), (c, c_out)))]
    for copy in copies:
        copy.start()
    for copy in copies:
        copy.wait()


def local(path_delta, assign, params, momentum):
    x_sum = path_delta[0].reshape(2, 16, 8, 8, 128).transpose(0, 1, 3, 2, 4)
    x_send = x_sum.reshape(2, 16, 8, 4, 2, 128)
    x_sum = x_sum.reshape(256, 8, 128)

    def rows_of(a):
        return a.reshape(MODULES, 2, 8, 128).transpose(0, 2, 1, 3).reshape(MODULES, 16, 128)

    def back(a):
        return a.reshape(MODULES, 8, 2, 128).transpose(0, 2, 1, 3).reshape(MODULES, 1, 2, 1024)

    any_space = pl.BlockSpec(memory_space=pl.ANY)
    vm = pltpu.VMEM
    slab = (MODULES, 16, 128)
    dma = pltpu.SemaphoreType.DMA
    operands = (x_send, x_sum, assign.T, rows_of(params[:, 0]), rows_of(momentum[:, 0]))
    ret, newp, newm = pl.pallas_call(
        kernel,
        out_shape=(
            jax.ShapeDtypeStruct((2, 16, 8, 4, 2, 128), f32),
            jax.ShapeDtypeStruct(slab, f32),
            jax.ShapeDtypeStruct(slab, f32),
        ),
        in_specs=[any_space] * 5,
        out_specs=[any_space] * 3,
        scratch_shapes=[
            vm((LEVELS, PATHS), i32), vm((256, 8, 128), f32), vm(slab, f32), vm(slab, f32), vm(slab, f32), vm(slab, f32),
            vm((CHUNKS, PATHS, LEVELS, WIDE, 2, 128), f32), vm((CHUNKS, LEVELS, PATHS + 1, SUB, 128), f32),
            vm((CHUNKS, PATHS, LEVELS, WIDE, 2, 128), f32),
            vm((1, 128), f32), vm((PATHS - 1, 1, 128), f32), vm((1, 128), f32), vm((SHARDS - 1, 1, 128), f32),
            vm((8, 128), i32), vm((8, 128), f32), vm((PATHS, 128), f32), pltpu.SMEM((8, 128), i32), pltpu.SMEM((8, 128), f32),
            dma((7,)), dma, dma, dma((SHARDS - 1,)), dma((SHARDS - 1,)), dma, dma((CHUNKS, PATHS)),
            dma((CHUNKS,)), dma((CHUNKS,)), dma((2 * CHUNKS,)),
        ],
        compiler_params=pltpu.CompilerParams(
            collective_id=1, has_side_effects=True, vmem_limit_bytes=32 * 2**20
        ),
        name="outer_step",
    )(*[pltpu.with_memory_space_constraint(v, pltpu.HBM) for v in operands])
    outs = (ret.reshape(2, 16, 8, 8, 128), newp, newm)
    ret, newp, newm = pl.pallas_call(
        finish,
        out_shape=[jax.ShapeDtypeStruct(o.shape, o.dtype) for o in outs],
        in_specs=[any_space] * 3,
        out_specs=[any_space] * 3,
        scratch_shapes=[dma((3,))],
        compiler_params=pltpu.CompilerParams(vmem_limit_bytes=2**20),
        name="finish",
    )(*[pltpu.with_memory_space_constraint(v, pltpu.VMEM) for v in outs])
    path_params = ret.transpose(0, 1, 3, 2, 4).reshape(1, 2, 128, 1024)
    return path_params, back(newp), back(newm)


def solution(mesh):
    in_specs = (
        P("path", None, "shard", None),
        P(),
        P(None, "shard", "path", None),
        P(None, "shard", "path", None),
    )
    out_specs = (
        P("path", None, "shard", None),
        P(None, "shard", "path", None),
        P(None, "shard", "path", None),
    )
    return jax.shard_map(local, mesh=mesh, in_specs=in_specs, out_specs=out_specs, check_vma=False)
```

```python
import jax
import jax.numpy as jnp
from jax import lax
from jax.experimental import pallas as pl
from jax.experimental.pallas import tpu as pltpu
from jax.sharding import PartitionSpec as P

LEVEL_MODULES = 16
LEVELS = 2
PATHS = 64
SHARDS = 4
MODULES = 32
CHUNKS = 2
EARLY = 63
GROUP = 16

outer_rate = 0.7
beta_coef = 0.9

MESH = pl.DeviceIdType.MESH
f32 = jnp.float32
i32 = jnp.int32
FIRST = (1,)
WIDE = 8 // CHUNKS
SUB = 2 * WIDE


def digits(p):
    return p // 16, p // 8 % 2, p // 2 % 4, p % 2


def links(offset):
    x, z, y, _ = digits(offset)
    ring = {0: (0, 0), 1: (1, 0), 2: (1, 1), 3: (0, 1)}
    return (*ring[x], *ring[y], z)


def far_first():
    left, load, order = list(range(1, PATHS)), (0,) * 5, [0]

    def cost(o):
        total = [a + b for a, b in zip(load, links(o))]
        return -sum(links(o)), max(total) - min(total), o * 45 % PATHS

    while left:
        o = min(left, key=cost)
        left.remove(o)
        order.append(o)
        load = tuple(a + b for a, b in zip(load, links(o)))
    return order


OFFSETS = far_first()


class Peers:
    def __init__(self, me):
        rem, div = lax.rem, lax.div
        x, z, y, c = div(me, 16), rem(div(me, 8), 2), rem(div(me, 2), 4), rem(me, 2)
        self.xs = [rem(x + d, 4) for d in range(4)]
        self.zs = [rem(z + d, 2) for d in range(2)]
        self.cs = [rem(c + d, 2) for d in range(2)]
        ys = [rem(y + d, 4) for d in range(4)]
        self.xz = [[a * 16 + b * 8 for b in self.zs] for a in self.xs]
        self.xz_tile = [[a * 4 + b * 2 for b in self.zs] for a in self.xs]
        self.yc = [[a * 2 + b for b in self.cs] for a in ys]
        self.y_tile = [div(a, 2) for a in ys]
        self.yc_pair = [[rem(a, 2) * 2 + b for b in self.cs] for a in ys]

    def to(self, i):
        dx, dz, dy, dc = digits(OFFSETS[i])
        return self.xz[dx][dz] + self.yc[dy][dc]

    def place(self, i):
        dx, dz, dy, dc = digits(OFFSETS[i])
        return self.xz_tile[dx][dz] + self.y_tile[dy], self.yc_pair[dy][dc]


def kernel(
    x_send, x_sum, assign_hbm, par_hbm, mom_hbm,
    ret_ref, newp_ref, newm_ref,
    assign_ref, xbuf, par, mom, newp, newm, landed, chain, outgoing, ahead,
    own_sq, sq_in, sq_row, sq_shards, itab, ftab, scale, itab_s, ftab_s,
    lsem, sq_send, sq_recv, sh_send, sh_recv, d_send, d_recv, r_send, r_recv, own_sem,
):
    me = lax.axis_index("path")
    shard = lax.axis_index("shard")
    peers = Peers(me)
    shard_peers = [lax.rem(shard + k, SHARDS) for k in range(SHARDS)]
    steps = range(1, PATHS)

    barrier = pltpu.get_barrier_semaphore()
    for i in steps[:32]:
        pl.semaphore_signal(barrier, inc=1, device_id=(peers.to(i), shard), device_id_type=MESH)
    for k in (2, 1, 3):
        pl.semaphore_signal(barrier, inc=1, device_id=(me, shard_peers[k]), device_id_type=MESH)
    for i in steps[32:]:
        pl.semaphore_signal(barrier, inc=1, device_id=(peers.to(i), shard), device_id_type=MESH)

    load_x = pltpu.make_async_copy(x_sum, xbuf, lsem.at[0])
    load_a = pltpu.make_async_copy(assign_hbm, assign_ref, lsem.at[3])
    load_p = pltpu.make_async_copy(par_hbm, par, lsem.at[1])
    load_m = pltpu.make_async_copy(mom_hbm, mom, lsem.at[2])
    for copy in (load_x, load_a, load_p, load_m):
        copy.start()

    load_a.wait()
    rows = lax.broadcasted_iota(i32, (PATHS, PATHS), 0)
    lanes = lax.broadcasted_iota(i32, (PATHS, PATHS), 1)
    x, z, y, c = lax.div(me, 16), lax.rem(lax.div(me, 8), 2), lax.rem(lax.div(me, 2), 4), lax.rem(me, 2)
    off = jnp.zeros((PATHS, PATHS), i32)
    for i in range(1, PATHS):
        off = jnp.where(rows == i, OFFSETS[i], off)
    frm = (
        ((x - (off >> 4)) & 3) * 16
        + ((z - ((off >> 3) & 1)) & 1) * 8
        + ((y - ((off >> 1) & 3)) & 3) * 2
        + ((c - (off & 1)) & 1)
    )
    for l in range(LEVELS):
        a_row = assign_ref[l : l + 1, :]
        a_col = jnp.sum(jnp.where(frm == lanes, jnp.broadcast_to(a_row, (PATHS, PATHS)), 0), axis=1, keepdims=True)
        a_mat = jnp.broadcast_to(a_col, (PATHS, PATHS))
        a_by_step = jnp.sum(jnp.where(rows == lanes, a_mat, 0), axis=0, keepdims=True)
        same = (a_mat == jnp.broadcast_to(a_by_step, (PATHS, PATHS))) & (rows < lanes)
        before = jnp.max(jnp.where(same, rows + 1, 0), axis=0, keepdims=True)
        mine = a_mat == lanes
        last = jnp.max(jnp.where(mine, rows + 1, 0), axis=0, keepdims=True)
        count = jnp.sum(jnp.where(mine, 1.0, 0.0).astype(f32), axis=0, keepdims=True)
        itab[l : l + 1, 0:PATHS] = before
        itab[2 + l : 3 + l, 0:PATHS] = last
        itab[4 + l : 5 + l, 0:PATHS] = a_row
        ftab[l : l + 1, 0:PATHS] = 1.0 / jnp.maximum(count, 1.0)
    ints = pltpu.make_async_copy(itab, itab_s, lsem.at[3])
    ints.start()
    floats = pltpu.make_async_copy(ftab, ftab_s, lsem.at[4])
    floats.start()

    load_x.wait()

    def square(i, acc):
        part = xbuf[pl.ds(i * 16, 16)]
        part = part * part
        return acc + jnp.sum(part.reshape(4, 4, 8, 128), axis=0)

    acc = lax.fori_loop(0, 16, square, jnp.zeros((4, 8, 128), f32))
    own_sq[...] = jnp.broadcast_to(jnp.sum(acc), (1, 128))
    for h in range(CHUNKS):
        for l in range(LEVELS):
            chain[h, l, 0] = jnp.zeros((SUB, 128), f32)
    ints.wait()
    floats.wait()

    pl.semaphore_wait(barrier, PATHS - 1 + SHARDS - 1)

    for i in steps:
        pltpu.make_async_remote_copy(
            own_sq, sq_in.at[i - 1], sq_send, sq_recv, device_id=(peers.to(i), shard), device_id_type=MESH
        ).start()

    def send_delta(h, i):
        tile, pair = peers.place(i)
        pltpu.make_async_remote_copy(
            x_send.at[:, tile, pl.ds(h * WIDE, WIDE), pair], landed.at[h, i], d_send, d_recv.at[h, i],
            device_id=(peers.to(i), shard), device_id_type=MESH,
        ).start()

    order = [(h, i) for h in range(CHUNKS) for i in steps]
    for h, i in order[:EARLY]:
        send_delta(h, i)
    tile, pair = peers.place(0)
    own = [
        pltpu.make_async_copy(x_send.at[:, tile, pl.ds(h * WIDE, WIDE), pair], landed.at[h, 0], own_sem.at[h])
        for h in range(CHUNKS)
    ]
    for copy in own:
        copy.start()

    pltpu.make_async_copy(sq_in, sq_in, sq_recv).wait()
    lane = lax.broadcasted_iota(i32, (1, 128), 1)
    part = [jnp.where(lane == 0, own_sq[...], 0.0)] + [jnp.where(lane == i, sq_in[i - 1], 0.0) for i in steps]
    while len(part) > 1:
        part = [a + b for a, b in zip(part[::2], part[1::2])]
    row = part[0]
    sq_row[...] = row
    copies = [
        pltpu.make_async_remote_copy(
            sq_row, sq_shards.at[k - 1], sh_send.at[k - 1], sh_recv.at[k - 1],
            device_id=(me, shard_peers[k]), device_id_type=MESH,
        )
        for k in range(1, SHARDS)
    ]
    for copy in copies:
        copy.start()
    for h, i in order[EARLY:]:
        send_delta(h, i)
    for copy in copies:
        copy.wait_recv()
    norm = row + sq_shards[0] + sq_shards[1] + sq_shards[2]
    rescale = 1.0 / jnp.sqrt(norm / (LEVELS * 512 * 1024) + 1e-06)
    spread = jnp.where(rows == lanes, jnp.broadcast_to(rescale[:, 0:PATHS], (PATHS, PATHS)), 0.0)
    scale[...] = jnp.broadcast_to(jnp.sum(spread, axis=1, keepdims=True), (PATHS, 128))
    load_p.wait()
    load_m.wait()

    arrived = landed.reshape(CHUNKS, PATHS, LEVELS, SUB, 128)
    ahead_view = ahead.reshape(len(FIRST), LEVELS, SUB, 128)
    out_view = outgoing.reshape(CHUNKS, PATHS, LEVELS, SUB, 128)
    my_tile, my_pair = peers.place(0)

    for h in range(CHUNKS):
        for i in range(PATHS):
            if i == 0:
                own[h].wait()
            else:
                pltpu.make_async_copy(landed.at[h, i], landed.at[h, i], d_recv.at[h, i]).wait()
            s = scale[i : i + 1, :]
            for l in range(LEVELS):
                chain[h, l, i + 1] = arrived[h, i, l] * s + chain[h, l, itab_s[l, i]]

        cols = pl.ds(h * SUB, SUB)
        for l in range(LEVELS):
            for m in range(LEVEL_MODULES):
                k = l * LEVEL_MODULES + m
                grad = chain[h, l, itab_s[2 + l, m]] * ftab_s[l, m]
                moment = beta_coef * mom[k, cols] + grad
                newm[k, cols] = moment
                newp[k, cols] = par[k, cols] - outer_rate * (grad + beta_coef * moment)

        def pick(i):
            to = peers.to(i)
            for l in range(LEVELS):
                out_view[h, i, l] = newp[l * LEVEL_MODULES + itab_s[4 + l, to], cols]

        def send_back(i):
            dst = ret_ref.at[:, my_tile, pl.ds(h * WIDE, WIDE), my_pair]
            if i == 0:
                pltpu.make_async_copy(outgoing.at[h, i], dst, own_sem.at[CHUNKS + h]).start()
            else:
                to = peers.to(i)
                copy = pltpu.make_async_remote_copy(
                    outgoing.at[h, i], dst, r_send.at[h], r_recv.at[h], device_id=(to, shard), device_id_type=MESH
                )
                if h < CHUNKS - 1:
                    copy.start()
                else:
                    other = to != FIRST[0]
                    for p in FIRST[1:]:
                        other = jnp.logical_and(other, to != p)
                    pl.when(other)(copy.start)

        def pick_first():
            for n, p in enumerate(FIRST):
                for l in range(LEVELS):
                    ahead_view[n, l] = newp[l * LEVEL_MODULES + itab_s[4 + l, p], cols]

        def send_first():
            dst = ret_ref.at[:, my_tile, pl.ds(h * WIDE, WIDE), my_pair]
            for n, p in enumerate(FIRST):
                copy = pltpu.make_async_remote_copy(
                    ahead.at[n], dst, r_send.at[h], r_recv.at[h], device_id=(p, shard), device_id_type=MESH
                )
                pl.when(me != p)(copy.start)

        todo = [1 + i for i in range(PATHS - 1)] + [0]
        groups = [todo[g : g + GROUP] for g in range(0, PATHS, GROUP)]
        if h == CHUNKS - 1:
            pick_first()
        for g in range(len(groups) + 1):
            if g == 1 and h == CHUNKS - 1:
                send_first()
            for i in groups[g] if g < len(groups) else ():
                pick(i)
            for i in groups[g - 1] if g > 0 else ():
                send_back(i)

    put_p = pltpu.make_async_copy(newp, newp_ref, lsem.at[5])
    put_m = pltpu.make_async_copy(newm, newm_ref, lsem.at[6])
    put_p.start()
    put_m.start()
    for copy in copies:
        copy.wait_send()
    pltpu.make_async_copy(sq_in, sq_in, sq_send).wait()
    for h in range(CHUNKS):
        rest = outgoing.at[h, pl.ds(1, PATHS - 1)]
        pltpu.make_async_copy(rest, rest, d_send).wait()
    put_p.wait()
    put_m.wait()
    for h in range(CHUNKS):
        rest = outgoing.at[h, pl.ds(1, PATHS - 1)]
        pltpu.make_async_copy(outgoing.at[h, 0], outgoing.at[h, 0], own_sem.at[CHUNKS + h]).wait()
        pltpu.make_async_copy(rest, rest, r_send.at[h]).wait()
        pltpu.make_async_copy(rest, rest, r_recv.at[h]).wait()


def finish(a, b, c, a_out, b_out, c_out, sem):
    copies = [pltpu.make_async_copy(s, d, sem.at[k]) for k, (s, d) in enumerate(((a, a_out), (b, b_out), (c, c_out)))]
    for copy in copies:
        copy.start()
    for copy in copies:
        copy.wait()


def local(path_delta, assign, params, momentum):
    x_sum = path_delta[0].reshape(2, 16, 8, 8, 128).transpose(0, 1, 3, 2, 4)
    x_send = x_sum.reshape(2, 16, 8, 4, 2, 128)
    x_sum = x_sum.reshape(256, 8, 128)

    def rows_of(a):
        return a.reshape(MODULES, 2, 8, 128).transpose(0, 2, 1, 3).reshape(MODULES, 16, 128)

    def back(a):
        return a.reshape(MODULES, 8, 2, 128).transpose(0, 2, 1, 3).reshape(MODULES, 1, 2, 1024)

    any_space = pl.BlockSpec(memory_space=pl.ANY)
    vm = pltpu.VMEM
    slab = (MODULES, 16, 128)
    dma = pltpu.SemaphoreType.DMA
    operands = (x_send, x_sum, assign.T, rows_of(params[:, 0]), rows_of(momentum[:, 0]))
    ret, newp, newm = pl.pallas_call(
        kernel,
        out_shape=(
            jax.ShapeDtypeStruct((2, 16, 8, 4, 2, 128), f32),
            jax.ShapeDtypeStruct(slab, f32),
            jax.ShapeDtypeStruct(slab, f32),
        ),
        in_specs=[any_space] * 5,
        out_specs=[any_space] * 3,
        scratch_shapes=[
            vm((LEVELS, PATHS), i32), vm((256, 8, 128), f32), vm(slab, f32), vm(slab, f32), vm(slab, f32), vm(slab, f32),
            vm((CHUNKS, PATHS, LEVELS, WIDE, 2, 128), f32), vm((CHUNKS, LEVELS, PATHS + 1, SUB, 128), f32),
            vm((CHUNKS, PATHS, LEVELS, WIDE, 2, 128), f32), vm((len(FIRST), LEVELS, WIDE, 2, 128), f32),
            vm((1, 128), f32), vm((PATHS - 1, 1, 128), f32), vm((1, 128), f32), vm((SHARDS - 1, 1, 128), f32),
            vm((8, 128), i32), vm((8, 128), f32), vm((PATHS, 128), f32), pltpu.SMEM((8, 128), i32), pltpu.SMEM((8, 128), f32),
            dma((7,)), dma, dma, dma((SHARDS - 1,)), dma((SHARDS - 1,)), dma, dma((CHUNKS, PATHS)),
            dma((CHUNKS,)), dma((CHUNKS,)), dma((2 * CHUNKS,)),
        ],
        compiler_params=pltpu.CompilerParams(
            collective_id=1, has_side_effects=True, vmem_limit_bytes=32 * 2**20
        ),
        name="outer_step",
    )(*[pltpu.with_memory_space_constraint(v, pltpu.HBM) for v in operands])
    outs = (ret.reshape(2, 16, 8, 8, 128), newp, newm)
    ret, newp, newm = pl.pallas_call(
        finish,
        out_shape=[jax.ShapeDtypeStruct(o.shape, o.dtype) for o in outs],
        in_specs=[any_space] * 3,
        out_specs=[any_space] * 3,
        scratch_shapes=[dma((3,))],
        compiler_params=pltpu.CompilerParams(vmem_limit_bytes=2**20),
        name="finish",
    )(*[pltpu.with_memory_space_constraint(v, pltpu.VMEM) for v in outs])
    path_params = ret.transpose(0, 1, 3, 2, 4).reshape(1, 2, 128, 1024)
    return path_params, back(newp), back(newm)


def solution(mesh):
    in_specs = (
        P("path", None, "shard", None),
        P(),
        P(None, "shard", "path", None),
        P(None, "shard", "path", None),
    )
    out_specs = (
        P("path", None, "shard", None),
        P(None, "shard", "path", None),
        P(None, "shard", "path", None),
    )
    return jax.shard_map(local, mesh=mesh, in_specs=in_specs, out_specs=out_specs, check_vma=False)
```
